512 devices in a mesh: head: 8 (over y, core), seq: 64 (over x, z).
Axes of the slice: x: 4, y: 4, z: 16, core: 2. Of those that a mesh axis runs over, the one named last changes fastest.
Arguments:
- queries: bfloat16 [2, 32768, 8, 256], P(None, 'seq', 'head'), may hold values from -5 to 5
- key_rows: bfloat16 [2, 32768, 8, 256], P(None, 'seq', 'head'), may hold values from -5 to 5
- values: bfloat16 [2, 32768, 8, 256], P(None, 'seq', 'head'), may hold values from -6 to 6
- learn_rates: float32 [8, 2, 32768], P('head', None, 'seq'), may hold values from 0.02 to 0.6, as said below
- fast_gate: float32 [8, 256, 512], P('head'), may hold values from -0.375 to 0.375
- fast_down: float32 [8, 512, 256], P('head'), may hold values from -0.25 to 0.25
- fast_up: float32 [8, 256, 512], P('head'), may hold values from -0.375 to 0.375
- output_weight: bfloat16 [2048, 2048], P(None, ('head', 'seq')), may hold values from -0.125 to 0.125
Outputs:
- output: bfloat16 [2, 32768, 2048], P(None, 'seq', 'head')
The draws below stay inside these ranges and needn't reach their ends.
Inputs may be any that keep to these rules, and one draw needn't show every extreme that they name: `learn_rates`: learning rates are positive.
All inputs are finite; a program needn't handle non-finite values.
Results may differ from the reference program's by a relative error of at most 0.0095.
Values may be sent and summed in bfloat16 or wider, within the bound.
No kernel may reach another device: no remote copies, remote signals or barrier semaphores. Data moves between devices by JAX's collectives and lax.ppermute only.
A program may use at most 64 MiB of HBM per device.

```python
import math
import jax
import jax.numpy as jnp
from jax import lax

DH = 256
HID = 512
WINDOW = 256
SPANS = 2
SPAN_DEV = 512
HEADS = 8
D = 2048
SPAN = 32768


def drawn_pair(key):
    base_key = jax.random.fold_in(key, 7001)
    subkeys = jax.random.split(base_key, 2)
    full_shape = (SPANS, SPAN, HEADS, DH)
    query_part = jnp.clip(jax.random.normal(subkeys[0], full_shape, jnp.float32), -4.0, 4.0)
    key_part = jnp.clip(jax.random.normal(subkeys[1], full_shape, jnp.float32), -4.0, 4.0)
    return (query_part, key_part)


def draw_queries(key, part):
    return drawn_pair(key)[0].astype(jnp.bfloat16)


def draw_key_rows(key, part):
    return drawn_pair(key)[1].astype(jnp.bfloat16)


def draw_learn_rates(key, part):
    base_key = jax.random.fold_in(key, 7013)
    full_shape = (HEADS, SPANS, SPAN)
    levels = jnp.exp(jax.random.uniform(base_key, full_shape, jnp.float32, math.log(0.02), math.log(0.2)))
    ramp_up = jnp.exp(math.log(3.0) * jnp.arange(SPAN, dtype=jnp.float32) / (SPAN - 1))
    return (levels * ramp_up).astype(jnp.float32)


def block_scale(own_key, shape, pieces, smallest, top_value):
    gain = 1.0
    for dim, parts in pieces:
        steps = jax.random.uniform(jax.random.fold_in(jax.random.fold_in(own_key, 6), dim), (parts,), jnp.float32, smallest / len(pieces), top_value / len(pieces))
        gain = gain * jnp.repeat(jnp.exp(steps), shape[dim] // parts).reshape((-1,) + (1,) * (len(shape) - 1 - dim))
    return gain


def gaussian(own_key, dims, deviation, most, cuts=(), kind=jnp.bfloat16):
    entries = jax.random.normal(own_key, dims, jnp.float32) * deviation
    if len(cuts) > 0:
        entries = block_scale(own_key, dims, cuts, -0.22, 0.18) * entries
    return jnp.clip(entries, min=-most, max=most).astype(kind)


def setup_inputs(seed: int = 0) -> dict:
    streams_of = jax.random.split(jax.random.key(seed), 9)
    queries = draw_queries(jax.random.fold_in(streams_of[8], 71), 0)
    key_rows = draw_key_rows(jax.random.fold_in(streams_of[8], 71), 0)
    values = gaussian(streams_of[2], (SPANS, SPAN, HEADS, DH), 1.0, 6.0, ((1, 64), (2, 8)))
    learn_rates = draw_learn_rates(jax.random.fold_in(streams_of[8], 71), 0)
    fast_gate = gaussian(streams_of[4], (HEADS, DH, HID), DH ** -0.5, 0.375, ((0, 8),), jnp.float32)
    fast_down = gaussian(streams_of[5], (HEADS, HID, DH), HID ** -0.5, 0.25, ((0, 8),), jnp.float32)
    fast_up = gaussian(streams_of[6], (HEADS, DH, HID), DH ** -0.5, 0.375, ((0, 8),), jnp.float32)
    output_weight = gaussian(streams_of[7], (D, D), D ** -0.5, 0.125, ((1, 512),))
    return {"queries": queries, "key_rows": key_rows, "values": values, "learn_rates": learn_rates, "fast_gate": fast_gate, "fast_down": fast_down, "fast_up": fast_up, "output_weight": output_weight}


MOMENTUM = 0.9

def silu_slope(pre_act):
    sigmoid_value = jax.nn.sigmoid(pre_act)
    return sigmoid_value * (1.0 + pre_act * (1.0 - sigmoid_value))

def span_gradient(key_span, value_span, rate_span, current):
    gate_low, down_low, up_low = current
    pre_gate = jnp.dot(key_span, gate_low, preferred_element_type=jnp.float32)
    pre_up = jnp.dot(key_span, up_low, preferred_element_type=jnp.float32)
    hidden = (jax.nn.silu(pre_gate) * pre_up).astype(jnp.bfloat16)
    target = (-(rate_span[:, None] * value_span.astype(jnp.float32))).astype(jnp.bfloat16)
    grad_down = jnp.dot(hidden.T, target, preferred_element_type=jnp.float32)
    back_grad = jnp.dot(target, down_low.T, preferred_element_type=jnp.float32)
    grad_pre_gate = (back_grad * pre_up * silu_slope(pre_gate)).astype(jnp.bfloat16)
    grad_pre_up = (back_grad * jax.nn.silu(pre_gate)).astype(jnp.bfloat16)
    grad_gate = jnp.dot(key_span.T, grad_pre_gate, preferred_element_type=jnp.float32)
    grad_up = jnp.dot(key_span.T, grad_pre_up, preferred_element_type=jnp.float32)
    return (grad_gate, grad_down, grad_up)

def apply_fast(query_span, current):
    gate_low, down_low, up_low = current
    pre_gate = jnp.dot(query_span, gate_low, preferred_element_type=jnp.float32)
    pre_up = jnp.dot(query_span, up_low, preferred_element_type=jnp.float32)
    hidden = (jax.nn.silu(pre_gate) * pre_up).astype(jnp.bfloat16)
    fast = jnp.dot(hidden, down_low, preferred_element_type=jnp.float32)
    return fast * lax.rsqrt(lax.optimization_barrier(jnp.mean(fast * fast, axis=-1, keepdims=True)) + 1e-05)

def fast_head(query_head, key_head, value_head, rate_head, gate_init, down_init, up_init):
    clip_bound = 0.6 * math.sqrt(HID)
    weights = (gate_init, down_init, up_init)
    current = tuple((matrix.astype(jnp.bfloat16) for matrix in weights))
    momentum = None
    results = []
    for span_index in range(SPANS):
        gradient = span_gradient(key_head[span_index], value_head[span_index], rate_head[span_index], current)
        squares = jnp.sum(gradient[0] * gradient[0]) + jnp.sum(gradient[1] * gradient[1]) + jnp.sum(gradient[2] * gradient[2])
        factor = jnp.minimum(1.0, clip_bound / jnp.sqrt(squares + 1e-06))
        if momentum is None:
            momentum = tuple((factor * member for member in gradient))
        else:
            momentum = tuple((MOMENTUM * earlier + factor * member for earlier, member in zip(momentum, gradient)))
        weights = tuple((matrix - change for matrix, change in zip(weights, momentum)))
        current = tuple((matrix.astype(jnp.bfloat16) for matrix in weights))
        results.append(apply_fast(query_head[span_index], current))
    return jnp.stack(results)

def window_head(query_flat, key_flat, value_flat):
    length = query_flat.shape[0]
    block_size = SPAN_DEV
    pad_keys = jnp.concatenate([jnp.zeros((WINDOW, DH), key_flat.dtype), key_flat], axis=0)
    pad_values = jnp.concatenate([jnp.zeros((WINDOW, DH), value_flat.dtype), value_flat], axis=0)
    row_ids = jnp.arange(block_size, dtype=jnp.int32)[:, None]
    col_ids = jnp.arange(block_size + WINDOW, dtype=jnp.int32)[None, :]
    in_band = (col_ids > row_ids) & (col_ids <= row_ids + WINDOW)
    score_scale = 1.0 / math.sqrt(DH)

    def one_block(block_index):
        offset = (block_index * block_size).astype(jnp.int32)
        query_rows = lax.dynamic_slice_in_dim(query_flat, offset, block_size, 0)
        key_block = lax.dynamic_slice_in_dim(pad_keys, offset, block_size + WINDOW, 0)
        value_block = lax.dynamic_slice_in_dim(pad_values, offset, block_size + WINDOW, 0)
        scores = jnp.dot(query_rows, key_block.T, preferred_element_type=jnp.float32) * score_scale
        allowed = in_band & (offset + col_ids >= WINDOW)
        scores = jnp.where(allowed, scores, -1e+30)
        row_max = lax.optimization_barrier(jnp.max(scores, axis=1, keepdims=True))
        exponent = jnp.exp(scores - row_max)
        probability = (exponent / lax.optimization_barrier(jnp.sum(exponent, axis=1, keepdims=True))).astype(jnp.bfloat16)
        return jnp.dot(probability, value_block, preferred_element_type=jnp.float32)
    blocks_out = lax.map(one_block, jnp.arange(length // block_size, dtype=jnp.int32))
    return blocks_out.reshape(length, DH)

def reference(queries, key_rows, values, learn_rates, fast_gate, fast_down, fast_up, output_weight):
    length = SPANS * SPAN
    mixed_heads = []
    for head_index in range(HEADS):
        query_head = queries[:, :, head_index]
        key_head = key_rows[:, :, head_index]
        value_head = values[:, :, head_index]
        fast_out = fast_head(query_head, key_head, value_head, learn_rates[head_index], fast_gate[head_index], fast_down[head_index], fast_up[head_index])
        window_out = window_head(query_head.reshape(length, DH), key_head.reshape(length, DH), value_head.reshape(length, DH))
        mixed_heads.append((fast_out.reshape(length, DH) + window_out).astype(jnp.bfloat16))
    joined = jnp.concatenate(mixed_heads, axis=1)
    result = jnp.dot(joined, output_weight, preferred_element_type=jnp.float32).astype(jnp.bfloat16)
    return result.reshape(SPANS, SPAN, D)
```

```python
import math

import jax
import jax.numpy as jnp
from jax import lax
from jax.experimental import pallas as pl
from jax.experimental.pallas import tpu as pltpu
from jax.sharding import Mesh
from jax.sharding import PartitionSpec as P

WINDOW = 256
MOMENTUM = 0.9
TILE = 256
HEAD = ("y", "core")
SEQ = ("x", "z_hi", "z_lo")
SCOPED = pltpu.CompilerParams(vmem_limit_bytes=48 * 1024 * 1024)


def mm(left, right, dims):
    return lax.dot_general(left, right, (dims, ((), ())), preferred_element_type=jnp.float32)


def blocks_of(gate, down, up):
    halves = [slice(j * TILE, (j + 1) * TILE) for j in range(gate.shape[1] // TILE)]
    return [gate[:, h] for h in halves] + [down[h, :] for h in halves] + [up[:, h] for h in halves]


def clip_factor(total, clip_bound):
    return jnp.minimum(1.0, clip_bound / jnp.sqrt(total + 1e-06))


def factor_of(grad_ref, clip_bound):
    total = jnp.zeros((1, 1), jnp.float32)
    for t in range(grad_ref.shape[0] // TILE):
        piece = grad_ref[t * TILE : (t + 1) * TILE, :].astype(jnp.float32)
        total = total + jnp.sum(piece * piece, keepdims=True)
    return clip_factor(total, clip_bound)


def write_gradient(keys, values, rates, tiles, out_ref):
    count = len(tiles) // 3
    rate_column = jnp.transpose(jnp.broadcast_to(rates, (8, rates.shape[1])))[:, :1]
    target = (-(rate_column * values.astype(jnp.float32))).astype(jnp.bfloat16)
    for j in range(count):
        gate, down, up = tiles[j], tiles[count + j], tiles[2 * count + j]
        pre_gate = mm(keys, gate, ((1,), (0,)))
        pre_up = mm(keys, up, ((1,), (0,)))
        back = mm(target, down, ((1,), (1,)))
        sigmoid = jax.nn.sigmoid(pre_gate)
        silu = pre_gate * sigmoid
        hidden = (silu * pre_up).astype(jnp.bfloat16)
        slope = sigmoid * (1.0 + pre_gate * (1.0 - sigmoid))
        grad_pre_gate = (back * pre_up * slope).astype(jnp.bfloat16)
        grad_pre_up = (back * silu).astype(jnp.bfloat16)
        for place, left, right in (
            (j, keys, grad_pre_gate),
            (count + j, hidden, target),
            (2 * count + j, keys, grad_pre_up),
        ):
            out_ref[place * TILE : (place + 1) * TILE, :] = mm(left, right, ((0,), (0,))).astype(
                out_ref.dtype
            )


def fast_norm(queries, tiles):
    count = len(tiles) // 3
    fast = None
    for j in range(count):
        pre_gate = mm(queries, tiles[j], ((1,), (0,)))
        pre_up = mm(queries, tiles[2 * count + j], ((1,), (0,)))
        hidden = (pre_gate * jax.nn.sigmoid(pre_gate) * pre_up).astype(jnp.bfloat16)
        part = mm(hidden, tiles[count + j], ((1,), (0,)))
        fast = part if fast is None else fast + part
    return fast * lax.rsqrt(jnp.mean(fast * fast, axis=-1, keepdims=True) + 1e-05)


def first_gradient_kernel(keys_ref, values_ref, rates_ref, gate_ref, down_ref, up_ref, out_ref):
    tiles = [t.astype(jnp.bfloat16) for t in blocks_of(gate_ref, down_ref, up_ref)]
    write_gradient(keys_ref[0], values_ref[0], rates_ref[0:1], tiles, out_ref)


def second_gradient_kernel(
    clip_bound, keys_ref, values_ref, rates_ref, gate_ref, down_ref, up_ref, grad_ref, out_ref, low_ref
):
    factor = factor_of(grad_ref, clip_bound)
    tiles = []
    for t, start in enumerate(blocks_of(gate_ref, down_ref, up_ref)):
        rows = slice(t * TILE, (t + 1) * TILE)
        low = (start - factor * grad_ref[rows, :].astype(jnp.float32)).astype(jnp.bfloat16)
        low_ref[rows, :] = low
        tiles.append(low)
    write_gradient(keys_ref[1], values_ref[1], rates_ref[1:2], tiles, out_ref)


def first_apply_kernel(queries_ref, low_ref, window_ref, out_ref):
    tiles = [low_ref[t * TILE : (t + 1) * TILE, :] for t in range(low_ref.shape[0] // TILE)]
    out_ref[...] = (fast_norm(queries_ref[0], tiles) + window_ref[0]).astype(out_ref.dtype)


def second_apply_kernel(
    clip_bound, queries_ref, gate_ref, down_ref, up_ref, first_ref, second_ref, window_ref, out_ref
):
    factor_first = factor_of(first_ref, clip_bound)
    factor_second = factor_of(second_ref, clip_bound)
    tiles = []
    for t, start in enumerate(blocks_of(gate_ref, down_ref, up_ref)):
        rows = slice(t * TILE, (t + 1) * TILE)
        momentum = factor_first * first_ref[rows, :].astype(jnp.float32)
        weights = start - momentum
        momentum = MOMENTUM * momentum + factor_second * second_ref[rows, :].astype(jnp.float32)
        tiles.append((weights - momentum).astype(jnp.bfloat16))
    out_ref[...] = (fast_norm(queries_ref[1], tiles) + window_ref[1]).astype(out_ref.dtype)


def window_kernel(first_ref, queries_ref, keys_ref, values_ref, edges_ref, out_ref):
    is_first = first_ref[0]
    spans, span_rows, head_dim = queries_ref.shape
    scale = 1.0 / math.sqrt(head_dim)
    shape = (WINDOW, 2 * WINDOW)
    row_ids = lax.broadcasted_iota(jnp.int32, shape, 0)
    col_ids = lax.broadcasted_iota(jnp.int32, shape, 1)
    in_band = (col_ids > row_ids) & (col_ids <= row_ids + WINDOW)
    for c in range(spans):
        edge_keys, edge_values = edges_ref[0, c], edges_ref[1, c]
        if c > 0:
            edge_keys = jnp.where(is_first == 1, edges_ref[0, c - 1], edge_keys)
            edge_values = jnp.where(is_first == 1, edges_ref[1, c - 1], edge_values)
        for start in range(0, span_rows, WINDOW):
            here = slice(start, start + WINDOW)
            before = slice(start - WINDOW, start)
            past_keys = keys_ref[c, before] if start else edge_keys
            past_values = values_ref[c, before] if start else edge_values
            query_rows = queries_ref[c, here]
            allowed = in_band
            if c == 0 and start == 0:
                allowed = in_band & (col_ids >= WINDOW * is_first)
            scores = jnp.concatenate(
                [
                    mm(query_rows, past_keys, ((1,), (1,))),
                    mm(query_rows, keys_ref[c, here], ((1,), (1,))),
                ],
                axis=1,
            )
            scores = jnp.where(allowed, scores * scale, -1e30)
            exponent = jnp.exp(scores - jnp.max(scores, axis=1, keepdims=True))
            probability = exponent / jnp.sum(exponent, axis=1, keepdims=True)
            probability = probability.astype(jnp.bfloat16)
            out_ref[c, here] = mm(probability[:, :WINDOW], past_values, ((1,), (0,))) + mm(
                probability[:, WINDOW:], values_ref[c, here], ((1,), (0,))
            )


def first_project_kernel(mixed_ref, weight_ref, out_ref):
    out_ref[...] = project(mixed_ref, weight_ref).astype(out_ref.dtype)


def project(mixed_ref, weight_ref):
    total = None
    for h in range(mixed_ref.shape[0]):
        width = mixed_ref.shape[2]
        part = mm(mixed_ref[h], weight_ref[:, h * width : (h + 1) * width], ((1,), (1,)))
        total = part if total is None else total + part
    return total


def whole(kernel, out_shape, *operands, name):
    return pl.pallas_call(kernel, out_shape=out_shape, compiler_params=SCOPED, name=name)(*operands)


def reduced(gradient):
    rows, width = gradient.shape
    pieces = lax.all_to_all(gradient.reshape(4, rows // 4, width), "x", 0, 0)
    part = jnp.sum(pieces.astype(jnp.float32), axis=0).astype(jnp.bfloat16)
    pieces = lax.all_to_all(part.reshape(4, rows // 16, width), "z_lo", 0, 0)
    part = jnp.sum(pieces.astype(jnp.float32), axis=0).astype(jnp.bfloat16)
    pieces = lax.all_gather(part, "z_hi")
    part = jnp.sum(pieces.astype(jnp.float32), axis=0).astype(jnp.bfloat16)
    part = lax.all_gather(part, "z_lo", tiled=True)
    return lax.all_gather(part, "x", tiled=True)


def body(queries, key_rows, values, learn_rates, fast_gate, fast_down, fast_up, output_weight):
    queries = queries[:, :, 0, :]
    keys = key_rows[:, :, 0, :]
    values = values[:, :, 0, :]
    rates = learn_rates[0]
    weights = (fast_gate[0], fast_down[0], fast_up[0])
    spans, span_rows, width = queries.shape
    hid = weights[0].shape[1]
    clip_bound = 0.6 * math.sqrt(hid)
    flat = jax.ShapeDtypeStruct((3 * hid, width), jnp.bfloat16)
    mixed_shape = jax.ShapeDtypeStruct((span_rows, width), jnp.bfloat16)

    local = whole(first_gradient_kernel, flat, keys, values, rates, *weights, name="grad_0")

    seq_count = lax.axis_size(SEQ)
    edges = lax.ppermute(
        jnp.stack([keys[:, span_rows - WINDOW :], values[:, span_rows - WINDOW :]]),
        SEQ,
        [(i, (i + 1) % seq_count) for i in range(seq_count)],
    )
    is_first = (lax.axis_index(SEQ) == 0).astype(jnp.int32).reshape(1)
    window = pl.pallas_call(
        window_kernel,
        out_shape=jax.ShapeDtypeStruct(queries.shape, jnp.float32),
        in_specs=[pl.BlockSpec(memory_space=pltpu.SMEM)]
        + [pl.BlockSpec(memory_space=pltpu.VMEM)] * 4,
        compiler_params=SCOPED,
        name="window",
    )(is_first, queries, keys, values, edges)
    weight_rows = lax.all_gather(output_weight.T, SEQ, axis=0, tiled=True)

    first = reduced(local)
    local, low = whole(
        lambda *refs: second_gradient_kernel(clip_bound, *refs),
        (flat, flat),
        keys,
        values,
        rates,
        *weights,
        first,
        name="grad_1",
    )
    mixed = whole(first_apply_kernel, mixed_shape, queries, low, window, name="apply_0")
    gathered_first = lax.all_gather(mixed, HEAD)
    second = reduced(local)
    mixed = whole(
        lambda *refs: second_apply_kernel(clip_bound, *refs),
        mixed_shape,
        queries,
        *weights,
        first,
        second,
        window,
        name="apply_1",
    )
    gathered_second = lax.all_gather(mixed, HEAD)

    def project_kernel(first_ref, second_ref, weight_ref, out_ref):
        out_ref[0] = project(first_ref, weight_ref).astype(out_ref.dtype)
        out_ref[1] = project(second_ref, weight_ref).astype(out_ref.dtype)

    return whole(
        project_kernel,
        jax.ShapeDtypeStruct((spans, span_rows, width), jnp.bfloat16),
        gathered_first,
        gathered_second,
        weight_rows,
        name="project",
    )


def solution(mesh):
    z = math.isqrt(mesh.shape["seq"] // 4)
    torus = Mesh(mesh.devices.reshape(mesh.shape["head"] // 2, 2, 4, z, z), HEAD + SEQ)
    placed = (
        P(None, SEQ, HEAD, None),
        P(None, SEQ, HEAD, None),
        P(None, SEQ, HEAD, None),
        P(HEAD, None, SEQ),
        P(HEAD, None, None),
        P(HEAD, None, None),
        P(HEAD, None, None),
        P(None, HEAD + SEQ),
    )
    return jax.shard_map(
        body, mesh=torus, in_specs=placed, out_specs=P(None, SEQ, HEAD), check_vma=False
    )
```
